512 devices in a mesh: row: 32 (over y, z_hi, core), col: 16 (over x, z_lo).
Axes of the slice: x: 4, y: 4, z: 16 (z_hi: 4, z_lo: 4; z = z_hi * 4 + z_lo), core: 2. Of those that a mesh axis runs over, the one named last changes fastest.
Arguments:
- inputs: bfloat16 [512, 8192], P('row', 'col'), may hold values from -6 to 6
- out_grad: bfloat16 [512, 8192], P('row', 'col'), may hold values from -1.5 to 1.5
- gate_weight: bfloat16 [8192, 16384], P('col', 'row'), may hold values from -0.0625 to 0.0625
- up_weight: bfloat16 [8192, 16384], P('col', 'row'), may hold values from -0.0625 to 0.0625
- down_weight: bfloat16 [16384, 8192], P('row', 'col'), may hold values from -0.046875 to 0.046875
Outputs:
- input_grad: bfloat16 [512, 8192], P('row', 'col')
- gate_weight_grad: bfloat16 [8192, 16384], P('col', 'row')
- up_weight_grad: bfloat16 [8192, 16384], P('col', 'row')
- down_weight_grad: bfloat16 [16384, 8192], P('row', 'col')
The draws below stay inside these ranges and needn't reach their ends.
All inputs are finite; a program needn't handle non-finite values.
Results may differ from the reference program's by a relative error of at most 0.0095.
Values may be sent and summed in bfloat16 or wider, within the bound.
A program may use at most 64 MiB of HBM per device.

```python
import jax
import jax.numpy as jnp

D = 8192
FF = 16384
TOKENS = 512


def level_of(stream_key, shape, split, least, largest):
    level, own = 1.0, jax.random.fold_in(stream_key, 6)
    for dim, blocks in split:
        draws = jnp.exp(jax.random.uniform(jax.random.fold_in(own, dim), (blocks,), jnp.float32, least / len(split), largest / len(split)))
        level = level * jnp.repeat(draws, shape[dim] // blocks).reshape([-1 if axis == dim else 1 for axis in range(len(shape))])
    return level


def normal_values(key, dims, width, most, pieces=(), held_as=jnp.bfloat16):
    factor_of = level_of(key, dims, pieces, -0.22, 0.18) if pieces else 1.0
    entries = jax.random.normal(key, dims, jnp.float32) * width * factor_of
    return jnp.minimum(jnp.maximum(entries, -most), most).astype(held_as)


def setup_inputs(seed: int = 0) -> dict:
    key_list = jax.random.split(jax.random.key(seed), 6)
    inputs = normal_values(key_list[0], (TOKENS, D), 1.0, 6.0, ((0, 32), (1, 16)))
    out_grad = normal_values(key_list[1], (TOKENS, D), 0.25, 1.5, ((0, 32), (1, 16)))
    gate_weight = normal_values(key_list[2], (D, FF), D ** -0.5, 0.0625, ((0, 16), (1, 32)))
    up_weight = normal_values(key_list[3], (D, FF), D ** -0.5, 0.0625, ((0, 16), (1, 32)))
    down_weight = normal_values(key_list[4], (FF, D), FF ** -0.5, 0.046875, ((0, 32), (1, 16)))
    return {"inputs": inputs, "out_grad": out_grad, "gate_weight": gate_weight, "up_weight": up_weight, "down_weight": down_weight}


def swiglu_back(gate, up_proj, hid_grad):
    sigma = jax.nn.sigmoid(gate)
    silu_gate = gate * sigma
    hidden = (silu_gate * up_proj).astype(jnp.bfloat16)
    up_grad = (hid_grad * silu_gate).astype(jnp.bfloat16)
    gate_grad = (hid_grad * up_proj * sigma * (1.0 + gate * (1.0 - sigma))).astype(jnp.bfloat16)
    return hidden, gate_grad, up_grad


def reference(inputs, out_grad, gate_weight, up_weight, down_weight):
    gate = jnp.dot(inputs, gate_weight, preferred_element_type=jnp.float32)
    up_proj = jnp.dot(inputs, up_weight, preferred_element_type=jnp.float32)
    hid_grad = jnp.dot(out_grad, down_weight.T, preferred_element_type=jnp.float32)
    hidden, gate_grad, up_grad = swiglu_back(gate, up_proj, hid_grad)
    down_weight_grad = jnp.dot(hidden.T, out_grad, preferred_element_type=jnp.float32).astype(jnp.bfloat16)
    gate_weight_grad = jnp.dot(inputs.T, gate_grad, preferred_element_type=jnp.float32).astype(jnp.bfloat16)
    up_weight_grad = jnp.dot(inputs.T, up_grad, preferred_element_type=jnp.float32).astype(jnp.bfloat16)
    input_grad = (jnp.dot(gate_grad, gate_weight.T, preferred_element_type=jnp.float32)
                  + jnp.dot(up_grad, up_weight.T, preferred_element_type=jnp.float32)).astype(jnp.bfloat16)
    return input_grad, gate_weight_grad, up_weight_grad, down_weight_grad
```

```python
import jax
import jax.numpy as jnp
from jax import lax
from jax.experimental import pallas as pl
from jax.experimental.pallas import tpu as pltpu
from jax.sharding import PartitionSpec as P

F32 = jnp.float32
BF16 = jnp.bfloat16
LAST = (((1,), (1,)), ((), ()))
ROWS = (((0,), (0,)), ((), ()))

Y_OFF = (0, 1, 3, 2)


class Sems:
    def __init__(self):
        self.names = {}

    def __getitem__(self, name):
        return self.names.setdefault(name, len(self.names))


N_SEMS = 160


def swiglu_back(gate, up_proj, hid_grad):
    sigma = jax.nn.sigmoid(gate)
    silu_gate = gate * sigma
    hidden = (silu_gate * up_proj).astype(BF16)
    up_grad = (hid_grad * silu_gate).astype(BF16)
    gate_grad = (hid_grad * up_proj * sigma * (1.0 + gate * (1.0 - sigma))).astype(BF16)
    return hidden, gate_grad, up_grad


def kernel(
    in_ref, og_ref, wg_ref, wu_ref, wd_ref,
    dx_ref, dwg_ref, dwu_ref, dwd_ref,
    XG, WG, WU, WD, PP, RX, Z, ZR, HGU, DXF, DXS, SR, YF, YS, YR, ZS, ZHR, OUT, DW,
    send_sem, recv_sem, local_sem,
):
    row = lax.axis_index("row")
    col = lax.axis_index("col")
    y, zh, core = row // 8, (row // 2) % 4, row % 2
    x, zl = col // 4, col % 4

    def at_row(yy, hh, cc):
        return (yy * 8 + hh * 2 + cc, col)

    def ypeer(d):
        return at_row((y + d) % 4, zh, core)

    def hpeer(d):
        return at_row(y, (zh + d) % 4, core)

    def xpeer(d):
        return (row, ((x + d) % 4) * 4 + zl)

    def lpeer(d):
        return (row, x * 4 + (zl + d) % 4)

    sib = at_row(y, zh, 1 - core)

    sems = Sems()
    pending = []

    def desc(name, src, dst, dev):
        i = sems[name]
        return pltpu.make_async_remote_copy(
            src_ref=src, dst_ref=dst, send_sem=send_sem.at[i], recv_sem=recv_sem.at[i],
            device_id=dev, device_id_type=pl.DeviceIdType.MESH,
        )

    started = {}

    def send(name, src, dst, dev):
        d = desc(name, src, dst, dev)
        d.start()
        started[name] = d

    def recv(name):
        started[name].wait_recv()

    loads = []
    for i, (src, dst) in enumerate((
        (in_ref, XG.at[0, 0, 0, 0]), (og_ref, XG.at[1, 0, 0, 0]),
        (wg_ref, WG), (wu_ref, WU), (wd_ref, WD),
    )):
        c = pltpu.make_async_copy(src, dst, local_sem.at[i])
        c.start()
        loads.append(c)

    barrier = pltpu.get_barrier_semaphore()
    peers = [sib] + [ypeer(d) for d in (1, 2, 3)] + [hpeer(d) for d in (1, 2, 3)]
    peers += [xpeer(1), xpeer(3)] + [lpeer(d) for d in (1, 2, 3)]
    for p in peers:
        pl.semaphore_signal(barrier, inc=1, device_id=p, device_id_type=pl.DeviceIdType.MESH)
    pl.semaphore_wait(barrier, len(peers))
    loads[0].wait()
    loads[1].wait()

    def spread(js, tag):
        src = XG.at[:, 0, 0, js]
        send("yp" + tag, src, XG.at[:, 2, 0, js], ypeer(1))
        send("ym" + tag, src, XG.at[:, 1, 0, js], ypeer(3))
        send("sib0" + tag, src, XG.at[:, 0, 1, js], sib)

    own = XG.at[:, 0, 0, 0]
    send("hp", own, XG.at[:, 0, 0, 2], hpeer(1))
    send("hm", own, XG.at[:, 0, 0, 1], hpeer(3))
    spread(pl.ds(0, 1), "0")
    recv("hp")
    send("hpp", XG.at[0, 0, 0, 2], XG.at[0, 0, 0, 3], hpeer(1))
    recv("hm")
    send("hmm", XG.at[1, 0, 0, 1], XG.at[1, 0, 0, 3], hpeer(3))
    spread(pl.ds(1, 2), "12")
    recv("hpp")
    recv("hmm")
    spread(pl.ds(3, 1), "3")
    tags = ("0", "12", "3")

    def a_near():
        for t in tags:
            recv("ym" + t)
        send("ymm", XG.at[1, 1, 0], XG.at[1, 3, 0], ypeer(3))
        send("sib1", XG.at[:, 1, 0], XG.at[:, 1, 1], sib)
        for t in tags:
            recv("yp" + t)
        send("ypp", XG.at[0, 2, 0], XG.at[0, 3, 0], ypeer(1))
        send("sib2", XG.at[:, 2, 0], XG.at[:, 2, 1], sib)

    def a_far():
        recv("ymm")
        recv("ypp")
        send("sib3", XG.at[:, 3, 0], XG.at[:, 3, 1], sib)

    xp, xm = (x + 1) % 4, (x + 3) % 4
    xf = (x + 2) % 4

    def s1(k):
        if k == 0:
            for t in tags:
                recv("sib0" + t)
            for c in loads[2:]:
                c.wait()
        else:
            recv("sib%d" % k)
        xk = XG[0, k].reshape(128, 512)
        gk = XG[1, k].reshape(128, 512)
        parts = (
            jnp.dot(xk, WG[...], preferred_element_type=F32),
            jnp.dot(xk, WU[...], preferred_element_type=F32),
            lax.dot_general(gk, WD[...], LAST, preferred_element_type=F32),
        )
        for i, part in enumerate(parts):
            part = part.astype(BF16)
            for q in range(4):
                PP[k, :, :, q, :, 128 * i:128 * (i + 1)] = (
                    part[:, 128 * q:128 * (q + 1)].reshape(4, 2, 16, 128))
        send("far+%d" % k, PP.at[k, xf, 0], RX.at[k, 0], xpeer(1))
        send("far-%d" % k, PP.at[k, xf, 1], RX.at[k, 1], xpeer(3))
        send("dir+%d" % k, PP.at[k, xp, 1], RX.at[k, 4], xpeer(1))
        send("dir-%d" % k, PP.at[k, xm, 0], RX.at[k, 3], xpeer(3))

    def s2(k):
        recv("far+%d" % k)
        PP[k, xp, 0] = (PP[k, xp, 0].astype(F32) + RX[k, 0].astype(F32)).astype(BF16)
        send("acc+%d" % k, PP.at[k, xp, 0], RX.at[k, 2], xpeer(1))
        recv("far-%d" % k)
        PP[k, xm, 1] = (PP[k, xm, 1].astype(F32) + RX[k, 1].astype(F32)).astype(BF16)
        send("acc-%d" % k, PP.at[k, xm, 1], RX.at[k, 5], xpeer(3))

    def s3(k):
        for n in ("dir+", "dir-", "acc+", "acc-"):
            recv(n + str(k))
        for h in range(2):
            Z[k, h] = (PP[k, x, h].astype(F32) + RX[k, 2 + 2 * h].astype(F32)
                       + RX[k, 3 + 2 * h].astype(F32)).astype(BF16)
        for m in (1, 2, 3):
            send("z%d%d" % (m, k), Z.at[k, :, (zl + m) % 4], ZR.at[k, m - 1], lpeer(m))

    def s4(k):
        for m in (1, 2, 3):
            recv("z%d%d" % (m, k))
        total = (Z[k, :, zl].astype(F32) + ZR[k, 0].astype(F32)
                 + ZR[k, 1].astype(F32) + ZR[k, 2].astype(F32))
        hidden, gate_grad, up_grad = swiglu_back(
            total[:, :, :128], total[:, :, 128:256], total[:, :, 256:])
        HGU[k, x, :, zl, :, 0:128] = hidden
        HGU[k, x, :, zl, :, 128:256] = gate_grad
        HGU[k, x, :, zl, :, 256:384] = up_grad
        for m in (1, 2, 3):
            mine = HGU.at[k, x, :, zl]
            send("g%d%d" % (m, k), mine, mine, lpeer(m))

    def s5(k):
        for m in (1, 2, 3):
            recv("g%d%d" % (m, k))
        mine = HGU.at[k, x]
        send("ag+%d" % k, mine, mine, xpeer(1))
        send("ag-%d" % k, mine, mine, xpeer(3))

    def s6(k):
        recv("ag+%d" % k)
        fwd = HGU.at[k, xm, 0]
        send("af+%d" % k, fwd, fwd, xpeer(1))
        recv("ag-%d" % k)
        fwd = HGU.at[k, xp, 1]
        send("af-%d" % k, fwd, fwd, xpeer(3))

    def cols(k, i):
        lead = (128,) if not isinstance(k, slice) else (512,)
        return jnp.concatenate(
            [HGU[k, :, :, q, :, 128 * i:128 * (i + 1)].reshape(lead + (128,)) for q in range(4)], axis=-1)

    def s7(k):
        recv("af+%d" % k)
        recv("af-%d" % k)
        dx = (lax.dot_general(cols(k, 1), WG[...], LAST, preferred_element_type=F32)
              + lax.dot_general(cols(k, 2), WU[...], LAST, preferred_element_type=F32))
        DXF[k] = dx[:64].reshape(4, 16, 512)
        DXS[k] = dx[64:].astype(BF16).reshape(4, 16, 512)
        send("f1%d" % k, DXS.at[k], SR.at[k], sib)

    def s8(k):
        recv("f1%d" % k)
        total = DXF[k] + SR[k].astype(F32)
        if k == 0:
            YF[...] = total
        else:
            YS[k - 1] = total.astype(BF16)
            send("f2%d" % k, YS.at[k - 1], YR.at[k - 1], ypeer(Y_OFF[k]))

    def s9():
        for k in (1, 2, 3):
            recv("f2%d" % k)
        total = YF[...] + YR[0].astype(F32) + YR[1].astype(F32) + YR[2].astype(F32)
        YF[...] = total
        for j, d in ((1, 1), (2, 3), (3, 2)):
            ZS[j - 1] = total[j].astype(BF16)
            send("f3%d" % j, ZS.at[j - 1], ZHR.at[j - 1], hpeer(d))

    def wgrads():
        al = slice(None)
        stores = []
        X = XG[0].reshape(512, 512)
        G = XG[1].reshape(512, 512)
        for i, (a, b, out) in enumerate((
            (cols(al, 0), G, dwd_ref), (X, cols(al, 1), dwg_ref), (X, cols(al, 2), dwu_ref),
        )):
            DW[i] = lax.dot_general(a, b, ROWS, preferred_element_type=F32).astype(BF16)
            c = pltpu.make_async_copy(DW.at[i], out, local_sem.at[5 + i])
            c.start()
            stores.append(c)
        return stores

    s1(0)
    a_near()
    s1(1)
    s2(0)
    s1(2)
    s2(1)
    a_far()
    s3(0)
    s1(3)
    s2(2)
    s3(1)
    s4(0)
    s2(3)
    s3(2)
    s4(1)
    s5(0)
    s3(3)
    s4(2)
    s5(1)
    s6(0)
    s4(3)
    s5(2)
    s6(1)
    s7(0)
    s5(3)
    s6(2)
    s7(1)
    s8(0)
    s6(3)
    s7(2)
    s8(1)
    s7(3)
    s8(2)
    s8(3)
    stores = wgrads()
    s9()
    for j in (1, 2, 3):
        recv("f3%d" % j)
    OUT[...] = (YF[0] + ZHR[0].astype(F32) + ZHR[1].astype(F32) + ZHR[2].astype(F32)).astype(BF16)
    c = pltpu.make_async_copy(OUT, dx_ref, local_sem.at[8])
    c.start()
    stores.append(c)
    for d in started.values():
        d.wait_send()
    for c in stores:
        c.wait()


def body(inputs, out_grad, gate_weight, up_weight, down_weight):
    any_spec = pl.BlockSpec(memory_space=pl.ANY)
    S = jax.ShapeDtypeStruct
    return tuple(pl.pallas_call(
        kernel,
        out_shape=(S((16, 512), BF16), S((512, 512), BF16), S((512, 512), BF16), S((512, 512), BF16)),
        in_specs=[any_spec] * 5,
        out_specs=(any_spec,) * 4,
        scratch_shapes=[
            pltpu.VMEM((2, 4, 2, 4, 16, 512), BF16),
            pltpu.VMEM((512, 512), BF16),
            pltpu.VMEM((512, 512), BF16),
            pltpu.VMEM((512, 512), BF16),
            pltpu.VMEM((4, 4, 2, 4, 16, 384), BF16),
            pltpu.VMEM((4, 6, 4, 16, 384), BF16),
            pltpu.VMEM((4, 2, 4, 16, 384), BF16),
            pltpu.VMEM((4, 3, 2, 16, 384), BF16),
            pltpu.VMEM((4, 4, 2, 4, 16, 384), BF16),
            pltpu.VMEM((4, 4, 16, 512), F32),
            pltpu.VMEM((4, 4, 16, 512), BF16),
            pltpu.VMEM((4, 4, 16, 512), BF16),
            pltpu.VMEM((4, 16, 512), F32),
            pltpu.VMEM((3, 4, 16, 512), BF16),
            pltpu.VMEM((3, 4, 16, 512), BF16),
            pltpu.VMEM((3, 16, 512), BF16),
            pltpu.VMEM((3, 16, 512), BF16),
            pltpu.VMEM((16, 512), BF16),
            pltpu.VMEM((3, 512, 512), BF16),
            pltpu.SemaphoreType.DMA((N_SEMS,)),
            pltpu.SemaphoreType.DMA((N_SEMS,)),
            pltpu.SemaphoreType.DMA((9,)),
        ],
        compiler_params=pltpu.CompilerParams(
            collective_id=0, has_side_effects=True, vmem_limit_bytes=48 * 1024 * 1024),
    )(inputs, out_grad, gate_weight, up_weight, down_weight))


def solution(mesh):
    placed = (P("row", "col"), P("row", "col"), P("col", "row"), P("col", "row"), P("row", "col"))
    return jax.shard_map(
        body,
        mesh=mesh,
        in_specs=placed,
        out_specs=(P("row", "col"), P("col", "row"), P("col", "row"), P("row", "col")),
        check_vma=False,
    )
```

```python
import jax
import jax.numpy as jnp
from jax import lax
from jax.experimental import pallas as pl
from jax.experimental.pallas import tpu as pltpu
from jax.sharding import PartitionSpec as P

F32 = jnp.float32
BF16 = jnp.bfloat16
ROWS = (((0,), (0,)), ((), ()))

OFF = (0, 1, 3, 2)


class Sems:
    def __init__(self):
        self.names = {}

    def __getitem__(self, name):
        return self.names.setdefault(name, len(self.names))


N_SEMS = 200


def swiglu_back(gate, up_proj, hid_grad):
    sigma = jax.nn.sigmoid(gate)
    silu_gate = gate * sigma
    hidden = (silu_gate * up_proj).astype(BF16)
    up_grad = (hid_grad * silu_gate).astype(BF16)
    gate_grad = (hid_grad * up_proj * sigma * (1.0 + gate * (1.0 - sigma))).astype(BF16)
    return hidden, gate_grad, up_grad


def kernel(
    in_ref, og_ref, wg_ref, wu_ref, wd_ref,
    dx_ref, dwg_ref, dwu_ref, dwd_ref,
    XG, WG, WU, WD, WGT, WUT, WDT, PP, RX, Z, ZR, HGU, DXF, DXS, SR, YF, ZS, ZHR, OUT, DW,
    send_sem, recv_sem, local_sem,
):
    row = lax.axis_index("row")
    col = lax.axis_index("col")
    y, zh, core = row // 8, (row // 2) % 4, row % 2
    x, zl = col // 4, col % 4

    def at_row(yy, hh, cc):
        return (yy * 8 + hh * 2 + cc, col)

    def ypeer(d, c=0):
        return at_row((y + d) % 4, zh, (core + c) % 2)

    def hpeer(d):
        return at_row(y, (zh + d) % 4, core)

    def xpeer(d):
        return (row, ((x + d) % 4) * 4 + zl)

    def lpeer(d):
        return (row, x * 4 + (zl + d) % 4)

    sib = at_row(y, zh, 1 - core)

    sems = Sems()
    def desc(name, src, dst, dev):
        i = sems[name]
        return pltpu.make_async_remote_copy(
            src_ref=src, dst_ref=dst, send_sem=send_sem.at[i], recv_sem=recv_sem.at[i],
            device_id=dev, device_id_type=pl.DeviceIdType.MESH,
        )

    started = {}

    def send(name, src, dst, dev):
        d = desc(name, src, dst, dev)
        d.start()
        started[name] = d

    def recv(name):
        started[name].wait_recv()

    loads = []
    for i, (src, dst) in enumerate((
        (in_ref, XG.at[0, 0, 0, 0]), (og_ref, XG.at[1, 0, 0, 0]),
        (wg_ref, WG), (wu_ref, WU), (wd_ref, WD),
    )):
        c = pltpu.make_async_copy(src, dst, local_sem.at[i])
        c.start()
        loads.append(c)

    barrier = pltpu.get_barrier_semaphore()
    peers = [sib] + [ypeer(d, c) for d in (1, 2, 3) for c in (0, 1)] + [hpeer(d) for d in (1, 2, 3)]
    peers += [xpeer(1), xpeer(3)] + [lpeer(d) for d in (1, 2, 3)]
    for p in peers:
        pl.semaphore_signal(barrier, inc=1, device_id=p, device_id_type=pl.DeviceIdType.MESH)
    pl.semaphore_wait(barrier, len(peers))
    loads[0].wait()
    loads[1].wait()

    NEG = (0, 2, 1, 3)

    def spread(k):
        src = XG.at[:, k, 0, 0]
        for c in (0, 1):
            for s in (1, 2, 3):
                send("y%d%d%d" % (k, c, s), src, XG.at[:, k, c, NEG[s]], ypeer(OFF[s], c))
        send("s%d" % k, src, XG.at[:, k, 1, 0], sib)

    spread(0)
    for s in (1, 2, 3):
        send("h%d" % s, XG.at[:, 0, 0, 0], XG.at[:, NEG[s], 0, 0], hpeer(OFF[s]))

    def a_z(k):
        recv("h%d" % NEG[k])
        spread(k)

    def weights():
        for c in loads[2:]:
            c.wait()
        WDT[...] = WD[...].T

    def weights2():
        WGT[...] = WG[...].T
        WUT[...] = WU[...].T

    xp, xm = (x + 1) % 4, (x + 3) % 4
    xf = (x + 2) % 4

    def s1(k):
        for c in (0, 1):
            for t in (1, 2, 3):
                recv("y%d%d%d" % (k, c, t))
        recv("s%d" % k)
        xk = XG[0, k].reshape(128, 512)
        gk = XG[1, k].reshape(128, 512)
        parts = (
            jnp.dot(xk, WG[...], preferred_element_type=F32),
            jnp.dot(xk, WU[...], preferred_element_type=F32),
            jnp.dot(gk, WDT[...], preferred_element_type=F32),
        )
        for i, part in enumerate(parts):
            part = part.astype(BF16)
            for q in range(4):
                PP[k, :, :, q, :, 128 * i:128 * (i + 1)] = (
                    part[:, 128 * q:128 * (q + 1)].reshape(4, 2, 16, 128))
        send("far+%d" % k, PP.at[k, xf, 0], RX.at[k, 0], xpeer(1))
        send("far-%d" % k, PP.at[k, xf, 1], RX.at[k, 1], xpeer(3))
        send("dir+%d" % k, PP.at[k, xp, 1], RX.at[k, 4], xpeer(1))
        send("dir-%d" % k, PP.at[k, xm, 0], RX.at[k, 3], xpeer(3))

    def s2(k):
        recv("far+%d" % k)
        PP[k, xp, 0] = (PP[k, xp, 0].astype(F32) + RX[k, 0].astype(F32)).astype(BF16)
        send("acc+%d" % k, PP.at[k, xp, 0], RX.at[k, 2], xpeer(1))
        recv("far-%d" % k)
        PP[k, xm, 1] = (PP[k, xm, 1].astype(F32) + RX[k, 1].astype(F32)).astype(BF16)
        send("acc-%d" % k, PP.at[k, xm, 1], RX.at[k, 5], xpeer(3))

    def s3(k):
        for n in ("dir+", "dir-", "acc+", "acc-"):
            recv(n + str(k))
        for h in range(2):
            Z[k, h] = (PP[k, x, h].astype(F32) + RX[k, 2 + 2 * h].astype(F32)
                       + RX[k, 3 + 2 * h].astype(F32)).astype(BF16)
        for m in (1, 2, 3):
            send("z%d%d" % (m, k), Z.at[k, :, (zl + m) % 4], ZR.at[k, m - 1], lpeer(m))

    def s4(k):
        for m in (1, 2, 3):
            recv("z%d%d" % (m, k))
        total = (Z[k, :, zl].astype(F32) + ZR[k, 0].astype(F32)
                 + ZR[k, 1].astype(F32) + ZR[k, 2].astype(F32))
        hidden, gate_grad, up_grad = swiglu_back(
            total[:, :, :128], total[:, :, 128:256], total[:, :, 256:])
        HGU[k, x, :, zl, :, 0:128] = hidden
        HGU[k, x, :, zl, :, 128:256] = gate_grad
        HGU[k, x, :, zl, :, 256:384] = up_grad
        for m in (1, 2, 3):
            mine = HGU.at[k, x, :, zl]
            send("g%d%d" % (m, k), mine, mine, lpeer(m))

    def s5(k):
        for m in (1, 2, 3):
            recv("g%d%d" % (m, k))
        mine = HGU.at[k, x]
        send("ag+%d" % k, mine, mine, xpeer(1))
        send("ag-%d" % k, mine, mine, xpeer(3))

    def s6(k):
        recv("ag+%d" % k)
        fwd = HGU.at[k, xm, 0]
        send("af+%d" % k, fwd, fwd, xpeer(1))
        recv("ag-%d" % k)
        fwd = HGU.at[k, xp, 1]
        send("af-%d" % k, fwd, fwd, xpeer(3))

    def cols(k, i):
        lead = (128,) if not isinstance(k, slice) else (512,)
        return jnp.concatenate(
            [HGU[k, :, :, q, :, 128 * i:128 * (i + 1)].reshape(lead + (128,)) for q in range(4)], axis=-1)

    def s7(k):
        recv("af+%d" % k)
        recv("af-%d" % k)
        dx = (jnp.dot(cols(k, 1), WGT[...], preferred_element_type=F32)
              + jnp.dot(cols(k, 2), WUT[...], preferred_element_type=F32))
        DXF[k] = dx[:16]
        DXS[k] = dx.astype(BF16).reshape(2, 4, 16, 512)
        for c in (0, 1):
            for s in (1, 2, 3):
                send("f%d%d%d" % (k, c, s), DXS.at[k, c, s], SR.at[k, c, NEG[s]], ypeer(OFF[s], c))
        send("f%d" % k, DXS.at[k, 1, 0], SR.at[k, 1, 0], sib)

    def s8(k):
        recv("f%d" % k)
        total = DXF[k] + SR[k, 1, 0].astype(F32)
        for c in (0, 1):
            for s in (1, 2, 3):
                recv("f%d%d%d" % (k, c, s))
                total += SR[k, c, NEG[s]].astype(F32)
        if k == 0:
            YF[...] = total
        else:
            ZS[k - 1] = total.astype(BF16)
            send("t%d" % k, ZS.at[k - 1], ZHR.at[k - 1], hpeer(OFF[k]))

    def s9():
        total = YF[...]
        for k in (1, 2, 3):
            recv("t%d" % k)
            total += ZHR[k - 1].astype(F32)
        OUT[...] = total.astype(BF16)
        c = pltpu.make_async_copy(OUT, dx_ref, local_sem.at[8])
        c.start()
        stores.append(c)

    stores = []

    def wgrad(i):
        al = slice(None)
        X = XG[0].reshape(512, 512)
        G = XG[1].reshape(512, 512)
        a, b, out = ((cols(al, 0), G, dwd_ref), (X, cols(al, 1), dwg_ref), (X, cols(al, 2), dwu_ref))[i]
        DW[i] = lax.dot_general(a, b, ROWS, preferred_element_type=F32).astype(BF16)
        c = pltpu.make_async_copy(DW.at[i], out, local_sem.at[5 + i])
        c.start()
        stores.append(c)

    stages = dict(
        s1=s1, s2=s2, s3=s3, s4=s4, s5=s5, s6=s6, s7=s7, s8=s8, s9=lambda _: s9(),
        az=a_z, w=lambda i: (weights, weights2)[i](), wg=wgrad,
    )
    for name, k in SCHED:
        stages[name](k)
    for d in started.values():
        d.wait_send()
    for c in stores:
        c.wait()


SCHED = (
    ("w", 0), ("s1", 0), ("az", 1), ("az", 2), ("s2", 0), ("az", 3), ("w", 1),
    ("s1", 1), ("s3", 0), ("s1", 2), ("s2", 1), ("s1", 3), ("s2", 2), ("s4", 0), ("s3", 1), ("s2", 3),
    ("s3", 2), ("s5", 0), ("s4", 1), ("s3", 3), ("s4", 2), ("s6", 0), ("s5", 1), ("s4", 3), ("s5", 2),
    ("s7", 0), ("s6", 1), ("s5", 3), ("s6", 2), ("s7", 1), ("s6", 3), ("s8", 0), ("s7", 2), ("s8", 1),
    ("s7", 3), ("wg", 0), ("s8", 2), ("s8", 3), ("wg", 1), ("wg", 2), ("s9", 0),
)


def body(inputs, out_grad, gate_weight, up_weight, down_weight):
    any_spec = pl.BlockSpec(memory_space=pl.ANY)
    S = jax.ShapeDtypeStruct
    return tuple(pl.pallas_call(
        kernel,
        out_shape=(S((16, 512), BF16), S((512, 512), BF16), S((512, 512), BF16), S((512, 512), BF16)),
        in_specs=[pl.BlockSpec(memory_space=pltpu.HBM)] * 5,
        out_specs=(any_spec,) * 4,
        scratch_shapes=[
            pltpu.VMEM((2, 4, 2, 4, 16, 512), BF16),
            pltpu.VMEM((512, 512), BF16),
            pltpu.VMEM((512, 512), BF16),
            pltpu.VMEM((512, 512), BF16),
            pltpu.VMEM((512, 512), BF16),
            pltpu.VMEM((512, 512), BF16),
            pltpu.VMEM((512, 512), BF16),
            pltpu.VMEM((4, 4, 2, 4, 16, 384), BF16),
            pltpu.VMEM((4, 6, 4, 16, 384), BF16),
            pltpu.VMEM((4, 2, 4, 16, 384), BF16),
            pltpu.VMEM((4, 3, 2, 16, 384), BF16),
            pltpu.VMEM((4, 4, 2, 4, 16, 384), BF16),
            pltpu.VMEM((4, 16, 512), F32),
            pltpu.VMEM((4, 2, 4, 16, 512), BF16),
            pltpu.VMEM((4, 2, 4, 16, 512), BF16),
            pltpu.VMEM((16, 512), F32),
            pltpu.VMEM((3, 16, 512), BF16),
            pltpu.VMEM((3, 16, 512), BF16),
            pltpu.VMEM((16, 512), BF16),
            pltpu.VMEM((3, 512, 512), BF16),
            pltpu.SemaphoreType.DMA((N_SEMS,)),
            pltpu.SemaphoreType.DMA((N_SEMS,)),
            pltpu.SemaphoreType.DMA((9,)),
        ],
        compiler_params=pltpu.CompilerParams(
            collective_id=0, has_side_effects=True, vmem_limit_bytes=60 * 1024 * 1024),
    )(inputs, out_grad, gate_weight, up_weight, down_weight))


def solution(mesh):
    placed = (P("row", "col"), P("row", "col"), P("col", "row"), P("col", "row"), P("row", "col"))
    return jax.shard_map(
        body,
        mesh=mesh,
        in_specs=placed,
        out_specs=(P("row", "col"), P("col", "row"), P("col", "row"), P("row", "col")),
        check_vma=False,
    )
```

```python
import jax
import jax.numpy as jnp
from jax import lax
from jax.experimental import pallas as pl
from jax.experimental.pallas import tpu as pltpu
from jax.sharding import PartitionSpec as P

F32 = jnp.float32
BF16 = jnp.bfloat16
ROWS = (((0,), (0,)), ((), ()))

OFF = (0, 1, 3, 2)
NEG = (0, 2, 1, 3)


class Sems:
    def __init__(self):
        self.names = {}

    def __getitem__(self, name):
        return self.names.setdefault(name, len(self.names))


N_SEMS = 320


def swiglu_back(gate, up_proj, hid_grad):
    sigma = jax.nn.sigmoid(gate)
    silu_gate = gate * sigma
    hidden = (silu_gate * up_proj).astype(BF16)
    up_grad = (hid_grad * silu_gate).astype(BF16)
    gate_grad = (hid_grad * up_proj * sigma * (1.0 + gate * (1.0 - sigma))).astype(BF16)
    return hidden, gate_grad, up_grad


def kernel(
    in_ref, og_ref, wg_ref, wu_ref, wd_ref,
    dx_ref, dwg_ref, dwu_ref, dwd_ref,
    XG, WG, WU, WD, WGT, WUT, WDT, PP, RX, Z, ZR, HGU, DXF, DXS, SR, YF, ZS, ZHR,
    send_sem, recv_sem, local_sem,
):
    row = lax.axis_index("row")
    col = lax.axis_index("col")
    y, zh, core = row // 8, (row // 2) % 4, row % 2
    x, zl = col // 4, col % 4

    def at_row(yy, hh, cc):
        return (yy * 8 + hh * 2 + cc, col)

    def ypeer(d, c=0):
        return at_row((y + d) % 4, zh, (core + c) % 2)

    def hpeer(d):
        return at_row(y, (zh + d) % 4, core)

    def xpeer(d):
        return (row, ((x + d) % 4) * 4 + zl)

    def lpeer(d):
        return (row, x * 4 + (zl + d) % 4)

    sib = at_row(y, zh, 1 - core)

    sems = Sems()
    def desc(name, src, dst, dev):
        i = sems[name]
        return pltpu.make_async_remote_copy(
            src_ref=src, dst_ref=dst, send_sem=send_sem.at[i], recv_sem=recv_sem.at[i],
            device_id=dev, device_id_type=pl.DeviceIdType.MESH,
        )

    started = {}

    def send(name, src, dst, dev):
        d = desc(name, src, dst, dev)
        d.start()
        started[name] = d

    def recv(name):
        started[name].wait_recv()

    loads = []
    for i, (src, dst) in enumerate((
        (in_ref, XG.at[0, 0, 0, 0]), (og_ref, XG.at[1, 0, 0, 0]),
        (wg_ref, WG), (wu_ref, WU), (wd_ref, WD),
    )):
        c = pltpu.make_async_copy(src, dst, local_sem.at[i])
        c.start()
        loads.append(c)

    barrier = pltpu.get_barrier_semaphore()
    peers = [sib] + [ypeer(d, c) for d in (1, 2, 3) for c in (0, 1)] + [hpeer(d) for d in (1, 3)]
    peers += [xpeer(d) for d in (1, 2, 3)] + [lpeer(d) for d in (1, 2, 3)]
    for p in peers:
        pl.semaphore_signal(barrier, inc=1, device_id=p, device_id_type=pl.DeviceIdType.MESH)
    pl.semaphore_wait(barrier, len(peers))
    loads[0].wait()
    loads[1].wait()


    def spread(k):
        src = XG.at[:, k, 0, 0]
        for c in (0, 1):
            for s in (1, 2, 3):
                send("y%d%d%d" % (k, c, s), src, XG.at[:, k, c, NEG[s]], ypeer(OFF[s], c))
        send("s%d" % k, src, XG.at[:, k, 1, 0], sib)

    spread(0)
    for s in (1, 2):
        send("h%d" % s, XG.at[:, 0, 0, 0], XG.at[:, NEG[s], 0, 0], hpeer(OFF[s]))

    def a_z(k):
        if k == 3:
            recv("h30")
            recv("h31")
        else:
            recv("h%d" % NEG[k])
        if k == 2:
            send("h30", XG.at[0, 2, 0, 0], XG.at[0, 3, 0, 0], hpeer(1))
        if k == 1:
            send("h31", XG.at[1, 1, 0, 0], XG.at[1, 3, 0, 0], hpeer(3))
        spread(k)

    def weights():
        for c in loads[2:]:
            c.wait()
        WDT[...] = WD[...].T

    def weights2():
        WGT[...] = WG[...].T
        WUT[...] = WU[...].T

    xp, xm = (x + 1) % 4, (x + 3) % 4
    xf = (x + 2) % 4

    def s1(k):
        for c in (0, 1):
            for t in (1, 2, 3):
                recv("y%d%d%d" % (k, c, t))
        recv("s%d" % k)
        xk = XG[0, k].reshape(128, 512)
        gk = XG[1, k].reshape(128, 512)
        parts = (
            jnp.dot(xk, WG[...], preferred_element_type=F32),
            jnp.dot(xk, WU[...], preferred_element_type=F32),
            jnp.dot(gk, WDT[...], preferred_element_type=F32),
        )
        for i, part in enumerate(parts):
            part = part.astype(BF16)
            for q in range(4):
                PP[k, :, :, q, :, 128 * i:128 * (i + 1)] = (
                    part[:, 128 * q:128 * (q + 1)].reshape(4, 2, 16, 128))
        send("far%d" % k, PP.at[k, xf], RX.at[k, 0], xpeer(2))
        send("dir+%d" % k, PP.at[k, xp], RX.at[k, 1], xpeer(1))
        send("dir-%d" % k, PP.at[k, xm], RX.at[k, 2], xpeer(3))

    def s3(k):
        for n in ("far", "dir+", "dir-"):
            recv(n + str(k))
        Z[k] = (PP[k, x].astype(F32) + RX[k, 0].astype(F32) + RX[k, 1].astype(F32)
                + RX[k, 2].astype(F32)).astype(BF16)
        for m in (1, 2, 3):
            send("z%d%d" % (m, k), Z.at[k, :, (zl + m) % 4], ZR.at[k, m - 1], lpeer(m))

    def s4(k):
        for m in (1, 2, 3):
            recv("z%d%d" % (m, k))
        total = (Z[k, :, zl].astype(F32) + ZR[k, 0].astype(F32)
                 + ZR[k, 1].astype(F32) + ZR[k, 2].astype(F32))
        hidden, gate_grad, up_grad = swiglu_back(
            total[:, :, :128], total[:, :, 128:256], total[:, :, 256:])
        HGU[k, x, :, zl, :, 0:128] = hidden
        HGU[k, x, :, zl, :, 128:256] = gate_grad
        HGU[k, x, :, zl, :, 256:384] = up_grad
        mine = HGU.at[k, x, :, zl]
        for m in (1, 2, 3):
            send("g%d%d" % (m, k), mine, mine, lpeer(m))

    def s5(k):
        for m in (1, 2, 3):
            recv("g%d%d" % (m, k))
        mine = HGU.at[k, x]
        send("ag%d" % k, mine, mine, xpeer(2))
        send("ag+%d" % k, mine, mine, xpeer(1))
        send("ag-%d" % k, mine, mine, xpeer(3))

    def cols(k, i):
        lead = (128,) if not isinstance(k, slice) else (512,)
        return jnp.concatenate(
            [HGU[k, :, :, q, :, 128 * i:128 * (i + 1)].reshape(lead + (128,)) for q in range(4)], axis=-1)

    def s7(k):
        for n in ("ag", "ag+", "ag-"):
            recv(n + str(k))
        dx = (jnp.dot(cols(k, 1), WGT[...], preferred_element_type=F32)
              + jnp.dot(cols(k, 2), WUT[...], preferred_element_type=F32))
        DXF[k] = dx[:16]
        DXS[k] = dx.astype(BF16).reshape(2, 4, 16, 512)
        for c in (0, 1):
            for s in (1, 2, 3):
                send("f%d%d%d" % (k, c, s), DXS.at[k, c, s], SR.at[k, c, NEG[s]], ypeer(OFF[s], c))
        send("f%d" % k, DXS.at[k, 1, 0], SR.at[k, 1, 0], sib)

    def s8(k):
        recv("f%d" % k)
        total = DXF[k] + SR[k, 1, 0].astype(F32)
        for c in (0, 1):
            for s in (1, 2, 3):
                recv("f%d%d%d" % (k, c, s))
                total += SR[k, c, NEG[s]].astype(F32)
        if k == 0:
            YF[...] = total
        else:
            ZS[k - 1] = total.astype(BF16)
            send("t%d" % k, ZS.at[k - 1], ZHR.at[k - 1], hpeer(OFF[k]))

    def s9():
        total = YF[...]
        for k in (1, 2, 3):
            recv("t%d" % k)
            total += ZHR[k - 1].astype(F32)
        dx_ref[...] = total.astype(BF16)

    def wgrad(i):
        al = slice(None)
        X = XG[0].reshape(512, 512)
        G = XG[1].reshape(512, 512)
        a, b, out = ((cols(al, 0), G, dwd_ref), (X, cols(al, 1), dwg_ref), (X, cols(al, 2), dwu_ref))[i]
        out[...] = lax.dot_general(a, b, ROWS, preferred_element_type=F32).astype(BF16)

    stages = dict(
        s1=s1, s3=s3, s4=s4, s5=s5, s7=s7, s8=s8, s9=lambda _: s9(),
        az=a_z, w=lambda i: (weights, weights2)[i](), wg=wgrad,
    )
    for name, k in SCHED:
        stages[name](k)
    for d in started.values():
        d.wait_send()


SCHED = (
    ("w", 0), ("s1", 0), ("az", 1), ("az", 2), ("az", 3), ("w", 1), ("s1", 1), ("s3", 0), ("s1", 2),
    ("s1", 3), ("s4", 0), ("s3", 1), ("s3", 2), ("s5", 0), ("s4", 1), ("s3", 3), ("s4", 2), ("s5", 1),
    ("s4", 3), ("s5", 2), ("s7", 0), ("s5", 3), ("s7", 1), ("s8", 0), ("s7", 2), ("s8", 1), ("s7", 3),
    ("wg", 0), ("s8", 2), ("s8", 3), ("wg", 1), ("wg", 2), ("s9", 0),
)


def copy_kernel(a, b, c, d, oa, ob, oc, od, sem):
    copies = [pltpu.make_async_copy(s, t, sem.at[i]) for i, (s, t) in enumerate(((a, oa), (b, ob), (c, oc), (d, od)))]
    for c in copies:
        c.start()
    for c in copies:
        c.wait()


def write_out(outs):
    any_spec = pl.BlockSpec(memory_space=pl.ANY)
    return tuple(pl.pallas_call(
        copy_kernel,
        out_shape=tuple(pltpu.HBM(o.shape, o.dtype) for o in outs),
        in_specs=[any_spec] * 4,
        out_specs=(any_spec,) * 4,
        scratch_shapes=[pltpu.SemaphoreType.DMA((4,))],
        name="write_out",
    )(*[pltpu.with_memory_space_constraint(o, pltpu.VMEM) for o in outs]))


def body(inputs, out_grad, gate_weight, up_weight, down_weight):
    args = [pltpu.with_memory_space_constraint(a, pltpu.HBM)
            for a in (inputs, out_grad, gate_weight, up_weight, down_weight)]
    outs = pl.pallas_call(
        kernel,
        out_shape=(pltpu.VMEM((16, 512), BF16),) + (pltpu.VMEM((512, 512), BF16),) * 3,
        in_specs=[pl.BlockSpec(memory_space=pl.ANY)] * 5,
        out_specs=(pl.BlockSpec(memory_space=pltpu.VMEM),) * 4,
        scratch_shapes=[
            pltpu.VMEM((2, 4, 2, 4, 16, 512), BF16),
            pltpu.VMEM((512, 512), BF16),
            pltpu.VMEM((512, 512), BF16),
            pltpu.VMEM((512, 512), BF16),
            pltpu.VMEM((512, 512), BF16),
            pltpu.VMEM((512, 512), BF16),
            pltpu.VMEM((512, 512), BF16),
            pltpu.VMEM((4, 4, 2, 4, 16, 384), BF16),
            pltpu.VMEM((4, 3, 2, 4, 16, 384), BF16),
            pltpu.VMEM((4, 2, 4, 16, 384), BF16),
            pltpu.VMEM((4, 3, 2, 16, 384), BF16),
            pltpu.VMEM((4, 4, 2, 4, 16, 384), BF16),
            pltpu.VMEM((4, 16, 512), F32),
            pltpu.VMEM((4, 2, 4, 16, 512), BF16),
            pltpu.VMEM((4, 2, 4, 16, 512), BF16),
            pltpu.VMEM((16, 512), F32),
            pltpu.VMEM((3, 16, 512), BF16),
            pltpu.VMEM((3, 16, 512), BF16),
            pltpu.SemaphoreType.DMA((N_SEMS,)),
            pltpu.SemaphoreType.DMA((N_SEMS,)),
            pltpu.SemaphoreType.DMA((5,)),
        ],
        compiler_params=pltpu.CompilerParams(
            collective_id=0, has_side_effects=True, vmem_limit_bytes=40 * 1024 * 1024),
    )(*args)
    return write_out(outs)


def solution(mesh):
    placed = (P("row", "col"), P("row", "col"), P("col", "row"), P("col", "row"), P("row", "col"))
    return jax.shard_map(
        body,
        mesh=mesh,
        in_specs=placed,
        out_specs=(P("row", "col"), P("col", "row"), P("col", "row"), P("row", "col")),
        check_vma=False,
    )
```

```python
import jax
import jax.numpy as jnp
from jax import lax
from jax.experimental import pallas as pl
from jax.experimental.pallas import tpu as pltpu
from jax.sharding import PartitionSpec as P

F32 = jnp.float32
BF16 = jnp.bfloat16
ROWS = (((0,), (0,)), ((), ()))

OFF = (0, 1, 3, 2)
NEG = (0, 2, 1, 3)


class Sems:
    def __init__(self):
        self.names = {}

    def __getitem__(self, name):
        return self.names.setdefault(name, len(self.names))


N_SEMS = 320


def swiglu_back(gate, up_proj, hid_grad):
    sigma = jax.nn.sigmoid(gate)
    silu_gate = gate * sigma
    hidden = (silu_gate * up_proj).astype(BF16)
    up_grad = (hid_grad * silu_gate).astype(BF16)
    gate_grad = (hid_grad * up_proj * sigma * (1.0 + gate * (1.0 - sigma))).astype(BF16)
    return hidden, gate_grad, up_grad


def kernel(
    in_ref, og_ref, wg_ref, wu_ref, wd_ref,
    dx_ref, dwg_ref, dwu_ref, dwd_ref,
    XG, WG, WU, WD, WGT, WUT, WDT, PP, RX, Z, ZR, HGU, DXF, DXS, SR, YF, ZS, ZHR,
    send_sem, recv_sem, local_sem,
):
    row = lax.axis_index("row")
    col = lax.axis_index("col")
    y, zh, core = row // 8, (row // 2) % 4, row % 2
    x, zl = col // 4, col % 4

    def at_row(yy, hh, cc):
        return (yy * 8 + hh * 2 + cc, col)

    def ypeer(d, c=0):
        return at_row((y + d) % 4, zh, (core + c) % 2)

    def hpeer(d):
        return at_row(y, (zh + d) % 4, core)

    def xpeer(d):
        return (row, ((x + d) % 4) * 4 + zl)

    def lpeer(d):
        return (row, x * 4 + (zl + d) % 4)

    sib = at_row(y, zh, 1 - core)

    sems = Sems()
    def desc(name, src, dst, dev):
        i = sems[name]
        return pltpu.make_async_remote_copy(
            src_ref=src, dst_ref=dst, send_sem=send_sem.at[i], recv_sem=recv_sem.at[i],
            device_id=dev, device_id_type=pl.DeviceIdType.MESH,
        )

    started = {}

    def send(name, src, dst, dev):
        d = desc(name, src, dst, dev)
        d.start()
        started[name] = d

    def recv(name):
        started[name].wait_recv()

    barrier = pltpu.get_barrier_semaphore()
    peers = [sib] + [ypeer(d, c) for d in (1, 2, 3) for c in (0, 1)] + [hpeer(d) for d in (1, 3)]
    peers += [xpeer(d) for d in (1, 2, 3)] + [lpeer(d) for d in (1, 2, 3)]
    for p in peers:
        pl.semaphore_signal(barrier, inc=1, device_id=p, device_id_type=pl.DeviceIdType.MESH)
    loads = []
    for i, (src, dst) in enumerate((
        (in_ref, XG.at[0, 0, 0, 0]), (og_ref, XG.at[1, 0, 0, 0]),
        (wg_ref, WG), (wu_ref, WU), (wd_ref, WD),
    )):
        c = pltpu.make_async_copy(src, dst, local_sem.at[i])
        c.start()
        loads.append(c)

    pl.semaphore_wait(barrier, len(peers))
    loads[0].wait()
    loads[1].wait()


    def spread(k):
        src = XG.at[:, k, 0, 0]
        for c in (0, 1):
            for s in (1, 2, 3):
                send("y%d%d%d" % (k, c, s), src, XG.at[:, k, c, NEG[s]], ypeer(OFF[s], c))
        send("s%d" % k, src, XG.at[:, k, 1, 0], sib)

    spread(0)
    for s in (1, 2):
        send("h%d" % s, XG.at[:, 0, 0, 0], XG.at[:, NEG[s], 0, 0], hpeer(OFF[s]))

    def a_z(k):
        if k == 3:
            recv("h30")
            recv("h31")
        else:
            recv("h%d" % NEG[k])
        if k == 2:
            send("h30", XG.at[0, 2, 0, 0], XG.at[0, 3, 0, 0], hpeer(1))
        if k == 1:
            send("h31", XG.at[1, 1, 0, 0], XG.at[1, 3, 0, 0], hpeer(3))
        spread(k)

    def weights():
        for c in loads[2:]:
            c.wait()
        WDT[...] = WD[...].T

    def weights2():
        WGT[...] = WG[...].T
        WUT[...] = WU[...].T

    xp, xm = (x + 1) % 4, (x + 3) % 4
    xf = (x + 2) % 4

    def s1(k):
        for c in (0, 1):
            for t in (1, 2, 3):
                recv("y%d%d%d" % (k, c, t))
        recv("s%d" % k)
        xk = XG[0, k].reshape(128, 512)
        gk = XG[1, k].reshape(128, 512)
        parts = (
            jnp.dot(xk, WG[...], preferred_element_type=F32),
            jnp.dot(xk, WU[...], preferred_element_type=F32),
            jnp.dot(gk, WDT[...], preferred_element_type=F32),
        )
        for i, part in enumerate(parts):
            part = part.astype(BF16)
            for q in range(4):
                PP[k, :, :, q, :, 128 * i:128 * (i + 1)] = (
                    part[:, 128 * q:128 * (q + 1)].reshape(4, 2, 16, 128))
        send("far%d" % k, PP.at[k, xf], RX.at[k, 0], xpeer(2))
        send("dir+%d" % k, PP.at[k, xp], RX.at[k, 1], xpeer(1))
        send("dir-%d" % k, PP.at[k, xm], RX.at[k, 2], xpeer(3))

    def s3(k):
        for n in ("far", "dir+", "dir-"):
            recv(n + str(k))
        Z[k] = (PP[k, x].astype(F32) + RX[k, 0].astype(F32) + RX[k, 1].astype(F32)
                + RX[k, 2].astype(F32)).astype(BF16)
        for m in (1, 2, 3):
            send("z%d%d" % (m, k), Z.at[k, :, (zl + m) % 4], ZR.at[k, m - 1], lpeer(m))

    def s4(k):
        for m in (1, 2, 3):
            recv("z%d%d" % (m, k))
        total = (Z[k, :, zl].astype(F32) + ZR[k, 0].astype(F32)
                 + ZR[k, 1].astype(F32) + ZR[k, 2].astype(F32))
        hidden, gate_grad, up_grad = swiglu_back(
            total[:, :, :128], total[:, :, 128:256], total[:, :, 256:])
        HGU[k, x, :, zl, :, 0:128] = hidden
        HGU[k, x, :, zl, :, 128:256] = gate_grad
        HGU[k, x, :, zl, :, 256:384] = up_grad
        mine = HGU.at[k, x, :, zl]
        for m in (1, 2, 3):
            send("g%d%d" % (m, k), mine, mine, lpeer(m))

    def s5(k):
        for m in (1, 2, 3):
            recv("g%d%d" % (m, k))
        mine = HGU.at[k, x]
        send("ag%d" % k, mine, mine, xpeer(2))
        send("ag+%d" % k, mine, mine, xpeer(1))
        send("ag-%d" % k, mine, mine, xpeer(3))

    def cols(k, i):
        lead = (128,) if not isinstance(k, slice) else (512,)
        return jnp.concatenate(
            [HGU[k, :, :, q, :, 128 * i:128 * (i + 1)].reshape(lead + (128,)) for q in range(4)], axis=-1)

    def s7(k):
        for n in ("ag", "ag+", "ag-"):
            recv(n + str(k))
        dx = (jnp.dot(cols(k, 1), WGT[...], preferred_element_type=F32)
              + jnp.dot(cols(k, 2), WUT[...], preferred_element_type=F32))
        DXF[k] = dx[:16]
        DXS[k] = dx.astype(BF16).reshape(2, 4, 16, 512)
        for c in (0, 1):
            for s in (1, 2, 3):
                send("f%d%d%d" % (k, c, s), DXS.at[k, c, s], SR.at[k, c, NEG[s]], ypeer(OFF[s], c))
        send("f%d" % k, DXS.at[k, 1, 0], SR.at[k, 1, 0], sib)

    def s8(k):
        recv("f%d" % k)
        total = DXF[k] + SR[k, 1, 0].astype(F32)
        for c in (0, 1):
            for s in (1, 2, 3):
                recv("f%d%d%d" % (k, c, s))
                total += SR[k, c, NEG[s]].astype(F32)
        if k == 0:
            YF[...] = total
        else:
            ZS[k - 1] = total.astype(BF16)
            send("t%d" % k, ZS.at[k - 1], ZHR.at[k - 1], hpeer(OFF[k]))

    def s9():
        total = YF[...]
        for k in (1, 2, 3):
            recv("t%d" % k)
            total += ZHR[k - 1].astype(F32)
        dx_ref[...] = total.astype(BF16)

    def wgrad(i):
        al = slice(None)
        X = XG[0].reshape(512, 512)
        G = XG[1].reshape(512, 512)
        a, b, out = ((cols(al, 0), G, dwd_ref), (X, cols(al, 1), dwg_ref), (X, cols(al, 2), dwu_ref))[i]
        out[...] = lax.dot_general(a, b, ROWS, preferred_element_type=F32).astype(BF16)

    stages = dict(
        s1=s1, s3=s3, s4=s4, s5=s5, s7=s7, s8=s8, s9=lambda _: s9(),
        az=a_z, w=lambda i: (weights, weights2)[i](), wg=wgrad,
    )
    for name, k in SCHED:
        stages[name](k)
    for d in started.values():
        d.wait_send()


SCHED = (
    ("w", 0), ("s1", 0), ("az", 1), ("az", 2), ("az", 3), ("w", 1), ("s1", 1), ("s3", 0), ("s1", 3),
    ("s1", 2), ("s4", 0), ("s3", 1), ("s3", 3), ("s5", 0), ("s4", 1), ("s3", 2), ("s4", 3), ("s5", 1),
    ("s4", 2), ("s5", 3), ("s7", 0), ("s5", 2), ("s7", 1), ("s8", 0), ("s7", 3), ("s8", 1), ("s7", 2),
    ("wg", 0), ("s8", 3), ("s8", 2), ("wg", 1), ("wg", 2), ("s9", 0),
)


def copy_kernel(a, b, c, d, oa, ob, oc, od, sem):
    copies = [pltpu.make_async_copy(s, t, sem.at[i]) for i, (s, t) in enumerate(((a, oa), (b, ob), (c, oc), (d, od)))]
    for c in copies:
        c.start()
    for c in copies:
        c.wait()


def write_out(outs):
    any_spec = pl.BlockSpec(memory_space=pl.ANY)
    return tuple(pl.pallas_call(
        copy_kernel,
        out_shape=tuple(pltpu.HBM(o.shape, o.dtype) for o in outs),
        in_specs=[any_spec] * 4,
        out_specs=(any_spec,) * 4,
        scratch_shapes=[pltpu.SemaphoreType.DMA((4,))],
        name="write_out",
    )(*[pltpu.with_memory_space_constraint(o, pltpu.VMEM) for o in outs]))


def body(inputs, out_grad, gate_weight, up_weight, down_weight):
    args = [pltpu.with_memory_space_constraint(a, pltpu.HBM)
            for a in (inputs, out_grad, gate_weight, up_weight, down_weight)]
    outs = pl.pallas_call(
        kernel,
        out_shape=(pltpu.VMEM((16, 512), BF16),) + (pltpu.VMEM((512, 512), BF16),) * 3,
        in_specs=[pl.BlockSpec(memory_space=pl.ANY)] * 5,
        out_specs=(pl.BlockSpec(memory_space=pltpu.VMEM),) * 4,
        scratch_shapes=[
            pltpu.VMEM((2, 4, 2, 4, 16, 512), BF16),
            pltpu.VMEM((512, 512), BF16),
            pltpu.VMEM((512, 512), BF16),
            pltpu.VMEM((512, 512), BF16),
            pltpu.VMEM((512, 512), BF16),
            pltpu.VMEM((512, 512), BF16),
            pltpu.VMEM((512, 512), BF16),
            pltpu.VMEM((4, 4, 2, 4, 16, 384), BF16),
            pltpu.VMEM((4, 3, 2, 4, 16, 384), BF16),
            pltpu.VMEM((4, 2, 4, 16, 384), BF16),
            pltpu.VMEM((4, 3, 2, 16, 384), BF16),
            pltpu.VMEM((4, 4, 2, 4, 16, 384), BF16),
            pltpu.VMEM((4, 16, 512), F32),
            pltpu.VMEM((4, 2, 4, 16, 512), BF16),
            pltpu.VMEM((4, 2, 4, 16, 512), BF16),
            pltpu.VMEM((16, 512), F32),
            pltpu.VMEM((3, 16, 512), BF16),
            pltpu.VMEM((3, 16, 512), BF16),
            pltpu.SemaphoreType.DMA((N_SEMS,)),
            pltpu.SemaphoreType.DMA((N_SEMS,)),
            pltpu.SemaphoreType.DMA((5,)),
        ],
        compiler_params=pltpu.CompilerParams(
            collective_id=0, has_side_effects=True, vmem_limit_bytes=40 * 1024 * 1024),
    )(*args)
    return write_out(outs)


def solution(mesh):
    placed = (P("row", "col"), P("row", "col"), P("col", "row"), P("col", "row"), P("row", "col"))
    return jax.shard_map(
        body,
        mesh=mesh,
        in_specs=placed,
        out_specs=(P("row", "col"), P("col", "row"), P("col", "row"), P("row", "col")),
        check_vma=False,
    )
```

```python
import jax
import jax.numpy as jnp
from jax import lax
from jax.experimental import pallas as pl
from jax.experimental.pallas import tpu as pltpu
from jax.sharding import PartitionSpec as P

F32 = jnp.float32
BF16 = jnp.bfloat16
ROWS = (((0,), (0,)), ((), ()))

OFF = (0, 1, 3, 2)
NEG = (0, 2, 1, 3)


class Sems:
    def __init__(self):
        self.names = {}

    def __getitem__(self, name):
        return self.names.setdefault(name, len(self.names))


N_SEMS = 320


def swiglu_back(gate, up_proj, hid_grad):
    sigma = jax.nn.sigmoid(gate)
    silu_gate = gate * sigma
    hidden = (silu_gate * up_proj).astype(BF16)
    up_grad = (hid_grad * silu_gate).astype(BF16)
    gate_grad = (hid_grad * up_proj * sigma * (1.0 + gate * (1.0 - sigma))).astype(BF16)
    return hidden, gate_grad, up_grad


def kernel(
    in_ref, og_ref, wg_ref, wu_ref, wd_ref,
    dx_ref, dwg_ref, dwu_ref, dwd_ref,
    XG, WG, WU, WD, WGT, WUT, WDT, PP, RX, Z, ZR, HGU, DXF, DXS, SR, YF, ZS, ZHR,
    send_sem, recv_sem, local_sem,
):
    row = lax.axis_index("row")
    col = lax.axis_index("col")
    y, zh, core = row // 8, (row // 2) % 4, row % 2
    x, zl = col // 4, col % 4

    def at_row(yy, hh, cc):
        return (yy * 8 + hh * 2 + cc, col)

    def ypeer(d, c=0):
        return at_row((y + d) % 4, zh, (core + c) % 2)

    def hpeer(d):
        return at_row(y, (zh + d) % 4, core)

    def xpeer(d):
        return (row, ((x + d) % 4) * 4 + zl)

    def lpeer(d):
        return (row, x * 4 + (zl + d) % 4)

    sib = at_row(y, zh, 1 - core)

    sems = Sems()
    def desc(name, src, dst, dev):
        i = sems[name]
        return pltpu.make_async_remote_copy(
            src_ref=src, dst_ref=dst, send_sem=send_sem.at[i], recv_sem=recv_sem.at[i],
            device_id=dev, device_id_type=pl.DeviceIdType.MESH,
        )

    started = {}

    def send(name, src, dst, dev):
        d = desc(name, src, dst, dev)
        d.start()
        started[name] = d

    def recv(name):
        started[name].wait_recv()

    barrier = pltpu.get_barrier_semaphore()
    peers = [sib] + [ypeer(d, c) for d in (1, 2, 3) for c in (0, 1)] + [hpeer(d) for d in (1, 3)]
    peers += [xpeer(d) for d in (1, 2, 3)] + [lpeer(d) for d in (1, 2, 3)]
    for p in peers:
        pl.semaphore_signal(barrier, inc=1, device_id=p, device_id_type=pl.DeviceIdType.MESH)
    loads = []
    for i, (src, dst) in enumerate((
        (in_ref, XG.at[0, 0, 0, 0]), (og_ref, XG.at[1, 0, 0, 0]),
        (wg_ref, WG), (wu_ref, WU), (wd_ref, WD),
    )):
        c = pltpu.make_async_copy(src, dst, local_sem.at[i])
        c.start()
        loads.append(c)

    pl.semaphore_wait(barrier, len(peers))
    loads[0].wait()
    loads[1].wait()


    def spread(k):
        src = XG.at[:, k, 0, 0]
        for c in (0, 1):
            for s in (1, 2, 3):
                send("y%d%d%d" % (k, c, s), src, XG.at[:, k, c, NEG[s]], ypeer(OFF[s], c))
        send("s%d" % k, src, XG.at[:, k, 1, 0], sib)

    spread(0)
    for s in (1, 2):
        send("h%d" % s, XG.at[:, 0, 0, 0], XG.at[:, NEG[s], 0, 0], hpeer(OFF[s]))

    def a_z(k):
        if k == 3:
            recv("h30")
            recv("h31")
        else:
            recv("h%d" % NEG[k])
        if k == 2:
            send("h30", XG.at[0, 2, 0, 0], XG.at[0, 3, 0, 0], hpeer(1))
        if k == 1:
            send("h31", XG.at[1, 1, 0, 0], XG.at[1, 3, 0, 0], hpeer(3))
        spread(k)

    def weights():
        for c in loads[2:]:
            c.wait()
        WDT[...] = WD[...].T

    def weights2():
        WGT[...] = WG[...].T
        WUT[...] = WU[...].T

    xp, xm = (x + 1) % 4, (x + 3) % 4
    xf = (x + 2) % 4

    def s1(g):
        k, u = g
        for t in (1, 2, 3):
            recv("y%d%d%d" % (k, u, t))
        if u:
            recv("s%d" % k)
        xk = XG[0, k, u].reshape(64, 512)
        gk = XG[1, k, u].reshape(64, 512)
        parts = (
            jnp.dot(xk, WG[...], preferred_element_type=F32),
            jnp.dot(xk, WU[...], preferred_element_type=F32),
            jnp.dot(gk, WDT[...], preferred_element_type=F32),
        )
        for i, part in enumerate(parts):
            part = part.astype(BF16)
            for q in range(4):
                PP[k, u, :, q, :, 128 * i:128 * (i + 1)] = (
                    part[:, 128 * q:128 * (q + 1)].reshape(4, 16, 128))
        send("far%d%d" % g, PP.at[k, u, xf], RX.at[k, u, 0], xpeer(2))
        send("dir+%d%d" % g, PP.at[k, u, xp], RX.at[k, u, 1], xpeer(1))
        send("dir-%d%d" % g, PP.at[k, u, xm], RX.at[k, u, 2], xpeer(3))

    def s3(g):
        k, u = g
        for n in ("far", "dir+", "dir-"):
            recv(n + "%d%d" % g)
        Z[k, u] = (PP[k, u, x].astype(F32) + RX[k, u, 0].astype(F32) + RX[k, u, 1].astype(F32)
                   + RX[k, u, 2].astype(F32)).astype(BF16)
        for m in (1, 2, 3):
            send("z%d%d%d" % (m, k, u), Z.at[k, u, (zl + m) % 4], ZR.at[k, u, m - 1], lpeer(m))

    def s4(g):
        k, u = g
        for m in (1, 2, 3):
            recv("z%d%d%d" % (m, k, u))
        total = (Z[k, u, zl].astype(F32) + ZR[k, u, 0].astype(F32)
                 + ZR[k, u, 1].astype(F32) + ZR[k, u, 2].astype(F32))
        hidden, gate_grad, up_grad = swiglu_back(total[:, :128], total[:, 128:256], total[:, 256:])
        HGU[k, u, x, zl, :, 0:128] = hidden
        HGU[k, u, x, zl, :, 128:256] = gate_grad
        HGU[k, u, x, zl, :, 256:384] = up_grad
        mine = HGU.at[k, u, x, zl]
        for m in (1, 2, 3):
            send("g%d%d%d" % (m, k, u), mine, mine, lpeer(m))

    def s5(g):
        k, u = g
        for m in (1, 2, 3):
            recv("g%d%d%d" % (m, k, u))
        mine = HGU.at[k, u, x]
        send("ag%d%d" % g, mine, mine, xpeer(2))
        send("ag+%d%d" % g, mine, mine, xpeer(1))
        send("ag-%d%d" % g, mine, mine, xpeer(3))

    def cols(i):
        return jnp.concatenate(
            [HGU[:, :, :, q, :, 128 * i:128 * (i + 1)].reshape(512, 128) for q in range(4)], axis=-1)

    def s7(g):
        k, u = g
        for n in ("ag", "ag+", "ag-"):
            recv(n + "%d%d" % g)
        gate_grad, up_grad = (
            jnp.concatenate(
                [HGU[k, u, :, q, :, 128 * i:128 * (i + 1)].reshape(64, 128) for q in range(4)], axis=-1)
            for i in (1, 2))
        dx = (jnp.dot(gate_grad, WGT[...], preferred_element_type=F32)
              + jnp.dot(up_grad, WUT[...], preferred_element_type=F32))
        if u == 0:
            DXF[k] = dx[:16]
        DXS[k, u] = dx.astype(BF16).reshape(4, 16, 512)
        for s in (1, 2, 3):
            send("f%d%d%d" % (k, u, s), DXS.at[k, u, s], SR.at[k, u, NEG[s]], ypeer(OFF[s], u))
        if u:
            send("f%d" % k, DXS.at[k, 1, 0], SR.at[k, 1, 0], sib)

    def s8(k):
        recv("f%d" % k)
        total = DXF[k] + SR[k, 1, 0].astype(F32)
        for c in (0, 1):
            for s in (1, 2, 3):
                recv("f%d%d%d" % (k, c, s))
                total += SR[k, c, NEG[s]].astype(F32)
        if k == 0:
            YF[...] = total
        else:
            ZS[k - 1] = total.astype(BF16)
            send("t%d" % k, ZS.at[k - 1], ZHR.at[k - 1], hpeer(OFF[k]))

    def s9():
        total = YF[...]
        for k in (1, 2, 3):
            recv("t%d" % k)
            total += ZHR[k - 1].astype(F32)
        dx_ref[...] = total.astype(BF16)

    def wgrad(i):
        X = XG[0].reshape(512, 512)
        G = XG[1].reshape(512, 512)
        a, b, out = ((cols(0), G, dwd_ref), (X, cols(1), dwg_ref), (X, cols(2), dwu_ref))[i]
        out[...] = lax.dot_general(a, b, ROWS, preferred_element_type=F32).astype(BF16)

    stages = dict(
        s1=s1, s3=s3, s4=s4, s5=s5, s7=s7, s8=s8, s9=lambda _: s9(),
        az=a_z, w=lambda i: (weights, weights2)[i](), wg=wgrad,
    )
    for name, k in SCHED:
        stages[name](k)
    for d in started.values():
        d.wait_send()


SCHED = (
    ("w", 0), ("w", 1), ("s1", (0, 0)), ("s1", (0, 1)), ("az", 2), ("az", 1), ("s1", (2, 0)), ("az", 3),
    ("s1", (2, 1)), ("s1", (1, 0)), ("s3", (2, 0)), ("s3", (0, 1)), ("s1", (3, 0)), ("s3", (2, 1)),
    ("s1", (3, 1)), ("s3", (1, 0)), ("s4", (0, 1)), ("s4", (2, 0)), ("s1", (1, 1)), ("s3", (3, 0)),
    ("s4", (2, 1)), ("s3", (0, 0)), ("s3", (3, 1)), ("s5", (0, 1)), ("s5", (2, 0)), ("s3", (1, 1)),
    ("s4", (3, 0)), ("s5", (2, 1)), ("s4", (0, 0)), ("s4", (3, 1)), ("s4", (1, 0)), ("s4", (1, 1)),
    ("s5", (3, 0)), ("s5", (3, 1)), ("s5", (1, 0)), ("s7", (2, 0)), ("s7", (0, 1)), ("s5", (1, 1)),
    ("s7", (3, 0)), ("s7", (2, 1)), ("s5", (0, 0)), ("s7", (3, 1)), ("s7", (1, 0)), ("s8", 3), ("s7", (1, 1)),
    ("s7", (0, 0)), ("s8", 2), ("s8", 1), ("wg", 2), ("wg", 0), ("wg", 1), ("s8", 0), ("s9", 0),
)


def copy_kernel(a, b, c, d, oa, ob, oc, od, sem):
    copies = [pltpu.make_async_copy(s, t, sem.at[i]) for i, (s, t) in enumerate(((a, oa), (b, ob), (c, oc), (d, od)))]
    for c in copies:
        c.start()
    for c in copies:
        c.wait()


def write_out(outs):
    any_spec = pl.BlockSpec(memory_space=pl.ANY)
    return tuple(pl.pallas_call(
        copy_kernel,
        out_shape=tuple(pltpu.HBM(o.shape, o.dtype) for o in outs),
        in_specs=[any_spec] * 4,
        out_specs=(any_spec,) * 4,
        scratch_shapes=[pltpu.SemaphoreType.DMA((4,))],
        name="write_out",
    )(*[pltpu.with_memory_space_constraint(o, pltpu.VMEM) for o in outs]))


def body(inputs, out_grad, gate_weight, up_weight, down_weight):
    args = [pltpu.with_memory_space_constraint(a, pltpu.HBM)
            for a in (inputs, out_grad, gate_weight, up_weight, down_weight)]
    outs = pl.pallas_call(
        kernel,
        out_shape=(pltpu.VMEM((16, 512), BF16),) + (pltpu.VMEM((512, 512), BF16),) * 3,
        in_specs=[pl.BlockSpec(memory_space=pl.ANY)] * 5,
        out_specs=(pl.BlockSpec(memory_space=pltpu.VMEM),) * 4,
        scratch_shapes=[
            pltpu.VMEM((2, 4, 2, 4, 16, 512), BF16),
            pltpu.VMEM((512, 512), BF16),
            pltpu.VMEM((512, 512), BF16),
            pltpu.VMEM((512, 512), BF16),
            pltpu.VMEM((512, 512), BF16),
            pltpu.VMEM((512, 512), BF16),
            pltpu.VMEM((512, 512), BF16),
            pltpu.VMEM((4, 2, 4, 4, 16, 384), BF16),
            pltpu.VMEM((4, 2, 3, 4, 16, 384), BF16),
            pltpu.VMEM((4, 2, 4, 16, 384), BF16),
            pltpu.VMEM((4, 2, 3, 16, 384), BF16),
            pltpu.VMEM((4, 2, 4, 4, 16, 384), BF16),
            pltpu.VMEM((4, 16, 512), F32),
            pltpu.VMEM((4, 2, 4, 16, 512), BF16),
            pltpu.VMEM((4, 2, 4, 16, 512), BF16),
            pltpu.VMEM((16, 512), F32),
            pltpu.VMEM((3, 16, 512), BF16),
            pltpu.VMEM((3, 16, 512), BF16),
            pltpu.SemaphoreType.DMA((N_SEMS,)),
            pltpu.SemaphoreType.DMA((N_SEMS,)),
            pltpu.SemaphoreType.DMA((5,)),
        ],
        compiler_params=pltpu.CompilerParams(
            collective_id=0, has_side_effects=True, vmem_limit_bytes=40 * 1024 * 1024),
    )(*args)
    return write_out(outs)


def solution(mesh):
    placed = (P("row", "col"), P("row", "col"), P("col", "row"), P("col", "row"), P("row", "col"))
    return jax.shard_map(
        body,
        mesh=mesh,
        in_specs=placed,
        out_specs=(P("row", "col"), P("col", "row"), P("col", "row"), P("row", "col")),
        check_vma=False,
    )
```

```python
import jax
import jax.numpy as jnp
from jax import lax
from jax.experimental import pallas as pl
from jax.experimental.pallas import tpu as pltpu
from jax.sharding import PartitionSpec as P

F32 = jnp.float32
BF16 = jnp.bfloat16
ROWS = (((0,), (0,)), ((), ()))

OFF = (0, 1, 3, 2)
NEG = (0, 2, 1, 3)


class Sems:
    def __init__(self):
        self.names = {}

    def __getitem__(self, name):
        return self.names.setdefault(name, len(self.names))


N_SEMS = 320


def swiglu_back(gate, up_proj, hid_grad):
    sigma = jax.nn.sigmoid(gate)
    silu_gate = gate * sigma
    hidden = (silu_gate * up_proj).astype(BF16)
    up_grad = (hid_grad * silu_gate).astype(BF16)
    gate_grad = (hid_grad * up_proj * sigma * (1.0 + gate * (1.0 - sigma))).astype(BF16)
    return hidden, gate_grad, up_grad


def kernel(
    in_ref, og_ref, wg_ref, wu_ref, wd_ref,
    dx_ref, dwg_ref, dwu_ref, dwd_ref,
    XG, WG, WU, WD, WGT, WUT, WDT, PP, RX, Z, ZR, HGU, DXF, DXS, SR, YF, ZS, ZHR,
    send_sem, recv_sem, local_sem,
):
    row = lax.axis_index("row")
    col = lax.axis_index("col")
    y, zh, core = row // 8, (row // 2) % 4, row % 2
    x, zl = col // 4, col % 4

    def at_row(yy, hh, cc):
        return (yy * 8 + hh * 2 + cc, col)

    def ypeer(d, c=0):
        return at_row((y + d) % 4, zh, (core + c) % 2)

    def hpeer(d):
        return at_row(y, (zh + d) % 4, core)

    def xpeer(d):
        return (row, ((x + d) % 4) * 4 + zl)

    def lpeer(d):
        return (row, x * 4 + (zl + d) % 4)

    sib = at_row(y, zh, 1 - core)

    sems = Sems()
    def desc(name, src, dst, dev):
        i = sems[name]
        return pltpu.make_async_remote_copy(
            src_ref=src, dst_ref=dst, send_sem=send_sem.at[i], recv_sem=recv_sem.at[i],
            device_id=dev, device_id_type=pl.DeviceIdType.MESH,
        )

    started = {}

    def send(name, src, dst, dev):
        d = desc(name, src, dst, dev)
        d.start()
        started[name] = d

    def recv(name):
        started[name].wait_recv()

    barrier = pltpu.get_barrier_semaphore()
    peers = [sib] + [ypeer(d, c) for d in (1, 2, 3) for c in (0, 1)] + [hpeer(d) for d in (1, 3)]
    peers += [xpeer(d) for d in (1, 2, 3)] + [lpeer(d) for d in (1, 2, 3)]
    for p in peers:
        pl.semaphore_signal(barrier, inc=1, device_id=p, device_id_type=pl.DeviceIdType.MESH)
    loads = []
    for i, (src, dst) in enumerate((
        (in_ref, XG.at[0, 0, 0, 0]), (og_ref, XG.at[1, 0, 0, 0]),
        (wg_ref, WG), (wu_ref, WU), (wd_ref, WD),
    )):
        c = pltpu.make_async_copy(src, dst, local_sem.at[i])
        c.start()
        loads.append(c)

    pl.semaphore_wait(barrier, len(peers))
    loads[0].wait()
    loads[1].wait()


    def spread(k):
        src = XG.at[:, k, 0, 0]
        for s in (1, 2, 3):
            send("y%d0%d" % (k, s), src, XG.at[:, k, 0, NEG[s]], ypeer(OFF[s]))
        send("s%d" % k, src, XG.at[:, k, 1, 0], sib)

    spread(0)
    for s in (1, 2):
        send("h%d" % s, XG.at[:, 0, 0, 0], XG.at[:, NEG[s], 0, 0], hpeer(OFF[s]))

    def a_z(k):
        if k == 3:
            recv("h30")
            recv("h31")
        else:
            recv("h%d" % NEG[k])
        if k == 2:
            send("h30", XG.at[0, 2, 0, 0], XG.at[0, 3, 0, 0], hpeer(1))
        if k == 1:
            send("h31", XG.at[1, 1, 0, 0], XG.at[1, 3, 0, 0], hpeer(3))
        spread(k)

    def weights():
        for c in loads[2:]:
            c.wait()
        WDT[...] = WD[...].T

    def weights2():
        WGT[...] = WG[...].T
        WUT[...] = WU[...].T

    xp, xm = (x + 1) % 4, (x + 3) % 4
    xf = (x + 2) % 4

    def s1(g):
        k, u = g
        if u:
            recv("rl%d" % k)
            recv("s%d" % k)
        else:
            for t in (1, 2, 3):
                recv("y%d0%d" % (k, t))
            send("rl%d" % k, XG.at[:, k, 0, pl.ds(1, 3)], XG.at[:, k, 1, pl.ds(1, 3)], sib)
        xk = XG[0, k, u].reshape(64, 512)
        gk = XG[1, k, u].reshape(64, 512)
        parts = (
            jnp.dot(xk, WG[...], preferred_element_type=F32),
            jnp.dot(xk, WU[...], preferred_element_type=F32),
            jnp.dot(gk, WDT[...], preferred_element_type=F32),
        )
        for i, part in enumerate(parts):
            part = part.astype(BF16)
            for q in range(4):
                PP[k, u, :, q, :, 128 * i:128 * (i + 1)] = (
                    part[:, 128 * q:128 * (q + 1)].reshape(4, 16, 128))
        send("far%d%d" % g, PP.at[k, u, xf], RX.at[k, u, 0], xpeer(2))
        send("dir+%d%d" % g, PP.at[k, u, xp], RX.at[k, u, 1], xpeer(1))
        send("dir-%d%d" % g, PP.at[k, u, xm], RX.at[k, u, 2], xpeer(3))

    def s3(g):
        k, u = g
        for n in ("far", "dir+", "dir-"):
            recv(n + "%d%d" % g)
        Z[k, u] = (PP[k, u, x].astype(F32) + RX[k, u, 0].astype(F32) + RX[k, u, 1].astype(F32)
                   + RX[k, u, 2].astype(F32)).astype(BF16)
        for m in (1, 2, 3):
            send("z%d%d%d" % (m, k, u), Z.at[k, u, (zl + m) % 4], ZR.at[k, u, m - 1], lpeer(m))

    def s4(g):
        k, u = g
        for m in (1, 2, 3):
            recv("z%d%d%d" % (m, k, u))
        total = (Z[k, u, zl].astype(F32) + ZR[k, u, 0].astype(F32)
                 + ZR[k, u, 1].astype(F32) + ZR[k, u, 2].astype(F32))
        hidden, gate_grad, up_grad = swiglu_back(total[:, :128], total[:, 128:256], total[:, 256:])
        HGU[k, u, x, zl, :, 0:128] = hidden
        HGU[k, u, x, zl, :, 128:256] = gate_grad
        HGU[k, u, x, zl, :, 256:384] = up_grad
        mine = HGU.at[k, u, x, zl]
        for m in (1, 2, 3):
            send("g%d%d%d" % (m, k, u), mine, mine, lpeer(m))

    def s5(g):
        k, u = g
        for m in (1, 2, 3):
            recv("g%d%d%d" % (m, k, u))
        mine = HGU.at[k, u, x]
        send("ag%d%d" % g, mine, mine, xpeer(2))
        send("ag+%d%d" % g, mine, mine, xpeer(1))
        send("ag-%d%d" % g, mine, mine, xpeer(3))

    def cols(i):
        return jnp.concatenate(
            [HGU[:, :, :, q, :, 128 * i:128 * (i + 1)].reshape(512, 128) for q in range(4)], axis=-1)

    def s7(g):
        k, u = g
        for n in ("ag", "ag+", "ag-"):
            recv(n + "%d%d" % g)
        gate_grad, up_grad = (
            jnp.concatenate(
                [HGU[k, u, :, q, :, 128 * i:128 * (i + 1)].reshape(64, 128) for q in range(4)], axis=-1)
            for i in (1, 2))
        dx = (jnp.dot(gate_grad, WGT[...], preferred_element_type=F32)
              + jnp.dot(up_grad, WUT[...], preferred_element_type=F32))
        if u == 0:
            DXF[k] = dx[:16]
        DXS[k, u] = dx.astype(BF16).reshape(4, 16, 512)
        for s in (1, 2, 3):
            send("f%d%d%d" % (k, u, s), DXS.at[k, u, s], SR.at[k, u, NEG[s]], ypeer(OFF[s], u))
        if u:
            send("f%d" % k, DXS.at[k, 1, 0], SR.at[k, 1, 0], sib)

    def s8(k):
        recv("f%d" % k)
        total = DXF[k] + SR[k, 1, 0].astype(F32)
        for c in (0, 1):
            for s in (1, 2, 3):
                recv("f%d%d%d" % (k, c, s))
                total += SR[k, c, NEG[s]].astype(F32)
        if k == 0:
            YF[...] = total
        else:
            ZS[k - 1] = total.astype(BF16)
            send("t%d" % k, ZS.at[k - 1], ZHR.at[k - 1], hpeer(OFF[k]))

    def s9():
        total = YF[...]
        for k in (1, 2, 3):
            recv("t%d" % k)
            total += ZHR[k - 1].astype(F32)
        dx_ref[...] = total.astype(BF16)

    def wgrad(i):
        X = XG[0].reshape(512, 512)
        G = XG[1].reshape(512, 512)
        a, b, out = ((cols(0), G, dwd_ref), (X, cols(1), dwg_ref), (X, cols(2), dwu_ref))[i]
        out[...] = lax.dot_general(a, b, ROWS, preferred_element_type=F32).astype(BF16)

    stages = dict(
        s1=s1, s3=s3, s4=s4, s5=s5, s7=s7, s8=s8, s9=lambda _: s9(),
        az=a_z, w=lambda i: (weights, weights2)[i](), wg=wgrad,
    )
    for name, k in SCHED:
        stages[name](k)
    for d in started.values():
        d.wait_send()


SCHED = (
    ("w", 0), ("w", 1), ("s1", (0, 0)), ("s1", (0, 1)), ("az", 2), ("az", 1), ("s1", (2, 0)), ("az", 3),
    ("s1", (2, 1)), ("s1", (1, 0)), ("s3", (2, 0)), ("s3", (0, 1)), ("s1", (3, 0)), ("s3", (2, 1)),
    ("s1", (3, 1)), ("s3", (1, 0)), ("s4", (0, 1)), ("s4", (2, 0)), ("s1", (1, 1)), ("s3", (3, 0)),
    ("s4", (2, 1)), ("s3", (0, 0)), ("s3", (3, 1)), ("s5", (0, 1)), ("s5", (2, 0)), ("s3", (1, 1)),
    ("s4", (3, 0)), ("s5", (2, 1)), ("s4", (0, 0)), ("s4", (3, 1)), ("s4", (1, 0)), ("s4", (1, 1)),
    ("s5", (3, 0)), ("s5", (3, 1)), ("s5", (1, 0)), ("s7", (2, 0)), ("s7", (0, 1)), ("s5", (1, 1)),
    ("s7", (3, 0)), ("s7", (2, 1)), ("s5", (0, 0)), ("s7", (3, 1)), ("s7", (1, 0)), ("s8", 3), ("s7", (1, 1)),
    ("s7", (0, 0)), ("s8", 2), ("s8", 1), ("wg", 2), ("wg", 0), ("wg", 1), ("s8", 0), ("s9", 0),
)


def copy_kernel(a, b, c, d, oa, ob, oc, od, sem):
    copies = [pltpu.make_async_copy(s, t, sem.at[i]) for i, (s, t) in enumerate(((a, oa), (b, ob), (c, oc), (d, od)))]
    for c in copies:
        c.start()
    for c in copies:
        c.wait()


def write_out(outs):
    any_spec = pl.BlockSpec(memory_space=pl.ANY)
    return tuple(pl.pallas_call(
        copy_kernel,
        out_shape=tuple(pltpu.HBM(o.shape, o.dtype) for o in outs),
        in_specs=[any_spec] * 4,
        out_specs=(any_spec,) * 4,
        scratch_shapes=[pltpu.SemaphoreType.DMA((4,))],
        name="write_out",
    )(*[pltpu.with_memory_space_constraint(o, pltpu.VMEM) for o in outs]))


def body(inputs, out_grad, gate_weight, up_weight, down_weight):
    args = [pltpu.with_memory_space_constraint(a, pltpu.HBM)
            for a in (inputs, out_grad, gate_weight, up_weight, down_weight)]
    outs = pl.pallas_call(
        kernel,
        out_shape=(pltpu.VMEM((16, 512), BF16),) + (pltpu.VMEM((512, 512), BF16),) * 3,
        in_specs=[pl.BlockSpec(memory_space=pl.ANY)] * 5,
        out_specs=(pl.BlockSpec(memory_space=pltpu.VMEM),) * 4,
        scratch_shapes=[
            pltpu.VMEM((2, 4, 2, 4, 16, 512), BF16),
            pltpu.VMEM((512, 512), BF16),
            pltpu.VMEM((512, 512), BF16),
            pltpu.VMEM((512, 512), BF16),
            pltpu.VMEM((512, 512), BF16),
            pltpu.VMEM((512, 512), BF16),
            pltpu.VMEM((512, 512), BF16),
            pltpu.VMEM((4, 2, 4, 4, 16, 384), BF16),
            pltpu.VMEM((4, 2, 3, 4, 16, 384), BF16),
            pltpu.VMEM((4, 2, 4, 16, 384), BF16),
            pltpu.VMEM((4, 2, 3, 16, 384), BF16),
            pltpu.VMEM((4, 2, 4, 4, 16, 384), BF16),
            pltpu.VMEM((4, 16, 512), F32),
            pltpu.VMEM((4, 2, 4, 16, 512), BF16),
            pltpu.VMEM((4, 2, 4, 16, 512), BF16),
            pltpu.VMEM((16, 512), F32),
            pltpu.VMEM((3, 16, 512), BF16),
            pltpu.VMEM((3, 16, 512), BF16),
            pltpu.SemaphoreType.DMA((N_SEMS,)),
            pltpu.SemaphoreType.DMA((N_SEMS,)),
            pltpu.SemaphoreType.DMA((5,)),
        ],
        compiler_params=pltpu.CompilerParams(
            collective_id=0, has_side_effects=True, vmem_limit_bytes=40 * 1024 * 1024),
    )(*args)
    return write_out(outs)


def solution(mesh):
    placed = (P("row", "col"), P("row", "col"), P("col", "row"), P("col", "row"), P("row", "col"))
    return jax.shard_map(
        body,
        mesh=mesh,
        in_specs=placed,
        out_specs=(P("row", "col"), P("col", "row"), P("col", "row"), P("row", "col")),
        check_vma=False,
    )
```
